32 devices in a mesh: ctx: 16 (over z, x, core), head: 2 (over y), ep: 1.
Axes of the slice: x: 2, y: 2, z: 4, core: 2. Of those that a mesh axis runs over, the one named last changes fastest.
Arguments:
- q_latent: bfloat16 [8192, 16, 576], P('ctx', ('head', 'ep')), may hold values from -20 to 20
- kv_latent: bfloat16 [8192, 576], P('ctx'), may hold values from -20 to 20
- w_value: bfloat16 [16, 512, 128], P(('head', 'ep')), may hold values from -0.25 to 0.25
- w_out: bfloat16 [2048, 2048], P(('head', 'ep')), may hold values from -0.125 to 0.125
- resid: bfloat16 [8192, 2048], P(('ctx', 'head', 'ep')), may hold values from -40 to 40
- norm_gain: float32 [2048], replicated, may hold values from 0.1 to 1.9
- w_gate: bfloat16 [16, 2048, 1408], P('ctx', None, 'head'), may hold values from -0.125 to 0.125
- w_up: bfloat16 [16, 2048, 1408], P('ctx', None, 'head'), may hold values from -0.125 to 0.125
- w_down_t: bfloat16 [16, 2048, 1408], P('ctx', None, 'head'), may hold values from -0.15625 to 0.15625
- expert_ids: int32 [8192, 6], P(('ctx', 'head', 'ep')), may hold values from 0 to 15, all different within a row; in each aligned block of 256 rows (0 to 255, 256 to 511, ...) at most 120 rows name the same one
- route_scores: float32 [8192, 6], P(('ctx', 'head', 'ep')), may hold values from 0.1 to 1
Outputs:
- layer_out: bfloat16 [8192, 2048], P(('ctx', 'head', 'ep'))
The draws below stay inside these ranges and needn't reach their ends.
Inputs may be any that keep to these rules, and one draw needn't show every extreme that they name: `expert_ids`: each row names 6 different experts. In each aligned block of 256 rows (the rows of one device) no expert is named by more than 120 rows, and in some block an expert is named by exactly 120 rows.
All inputs are finite; a program needn't handle non-finite values.
Results may differ from the reference program's by a relative error of at most 0.007.
Values may be sent and summed in bfloat16 or wider, within the bound.
No kernel may reach another device: no remote copies, remote signals or barrier semaphores. Data moves between devices by JAX's collectives and lax.ppermute only.
A program may use at most 256 MiB of HBM per device.

```python
import math
import jax
import jax.numpy as jnp
import numpy as np
from jax import lax

D = 2048
HEADS = 16
LAT = 512
ROPE = 64
NOPE = 128
VDIM = 128
FF = 1408
TOPK = 6
L = 8192
EXPERTS = 16
ROWS = 256
CAP = 120


def attention_pair(key):
    base_key = jax.random.fold_in(key, 7103)
    width_all = LAT + ROPE
    latents = jax.random.truncated_normal(jax.random.fold_in(base_key, 1), -4.0, 4.0, (L, width_all), jnp.float32)
    queries = jax.random.truncated_normal(jax.random.fold_in(base_key, 2), -4.0, 4.0, (L, HEADS, width_all), jnp.float32)
    return (jnp.clip(queries, -20.0, 20.0), jnp.clip(latents, -20.0, 20.0))


def draw_q_latent(key, part):
    return attention_pair(key)[0].astype(jnp.bfloat16)


def draw_kv_latent(key, part):
    return attention_pair(key)[1].astype(jnp.bfloat16)


def draw_resid(key, part):
    base_key = jax.random.fold_in(key, 9241)
    row_scale = jnp.exp(jax.random.uniform(jax.random.fold_in(base_key, 1), (L, 1), jnp.float32, minval=math.log(0.3), maxval=math.log(3.0)))
    column_scale = jnp.exp(jax.random.uniform(jax.random.fold_in(base_key, 2), (1, D), jnp.float32, minval=math.log(0.3), maxval=math.log(3.0)))
    values = jax.random.truncated_normal(jax.random.fold_in(base_key, 4), -4.0, 4.0, (L, D), jnp.float32)
    return (values * row_scale * column_scale).astype(jnp.bfloat16)


def level_of(stream_key, shape, split, low, top_value):
    loudness, own = 1.0, jax.random.fold_in(stream_key, 6)
    for axis_at, blocks in split:
        heights = jnp.exp(jax.random.uniform(jax.random.fold_in(own, axis_at), (blocks,), jnp.float32, low / len(split), top_value / len(split)))
        loudness = loudness * jnp.repeat(heights, shape[axis_at] // blocks).reshape([-1 if axis == axis_at else 1 for axis in range(len(shape))])
    return loudness


def assign_block(key, own, number, rows, number_of, top, reach, skew):
    order = jax.random.permutation(key, number_of)
    crowded, ordinary = load_shares(number_of, rows * top, reach, skew, True), load_shares(number_of, rows * top, reach, skew, False)
    places = jnp.arange(number_of)

    def named(lengths, rotation):
        used = int((lengths > 0).sum())
        fixed = max(1, used // 4)
        moved = fixed + (places - fixed + rotation * (used - fixed)) % max(1, number_of - fixed)
        return jnp.zeros((number_of,), jnp.int32).at[order[jnp.where(places < fixed, places, moved)]].set(jnp.asarray(lengths, jnp.int32))

    lengths = jnp.where(number % 4 == 0, named(crowded, number // 4), named(ordinary, number - number // 4 - 1))
    mixed = jax.random.permutation(jax.random.fold_in(own, 3), number_of)
    source_of, receiver = mixed[0:number_of // 2 * 2:2], mixed[1:number_of // 2 * 2:2]
    margin = jnp.minimum(lengths[source_of] - 1, reach - lengths[receiver]) // 2
    margin = jnp.where((source_of == order[0]) | (receiver == order[0]) | (lengths[receiver] == 0), 0, jnp.maximum(margin, 0))
    moved = jax.random.randint(jax.random.fold_in(own, 4), (number_of // 2,), 0, 1 << 20) % (margin + 1)
    lengths = lengths.at[source_of].add(-moved).at[receiver].add(moved)
    labels = jnp.searchsorted(jnp.cumsum(lengths), jnp.arange(rows * top), side="right").astype(jnp.int32)
    table = labels.reshape(top, rows).T
    table = table[jax.random.permutation(jax.random.fold_in(own, 1), rows)]
    rotation = jax.random.randint(jax.random.fold_in(own, 2), (rows, 1), 0, top)
    return jnp.take_along_axis(table, (jnp.arange(top)[None, :] + rotation) % top, axis=1)


def load_shares(amount, total, reach, lean, full):
    weights = [(1 << 20) // math.isqrt(standing ** lean) + 1 for standing in range(1, amount + 1)]
    largest = reach if full else min(reach, max(-(-total // amount), total * weights[0] // sum(weights)))
    least = 1 if total - largest >= amount - 1 else 0
    holding, spare = [largest] + [least] * (amount - 1), total - largest - least * (amount - 1)
    while spare > 0:
        candidates = [i for i in range(1, amount) if holding[i] < largest] or [i for i in range(1, amount) if holding[i] < reach]
        pool, remaining = sum([weights[i] for i in candidates]), spare
        for i in candidates:
            more = min(reach - holding[i], max(1, remaining * weights[i] // pool), spare)
            holding[i] = holding[i] + more
            spare = spare - more
    return np.array(holding)


def bell_draw(rng, shape, width, limit, cuts=(), kind=jnp.bfloat16):
    drawn = jax.random.normal(rng, shape, jnp.float32) * width
    if len(cuts) > 0:
        drawn = level_of(rng, shape, cuts, -0.22, 0.18) * drawn
    return jnp.clip(drawn, min=-limit, max=limit).astype(kind)


def setup_inputs(seed: int = 0) -> dict:
    seeds = jax.random.split(jax.random.key(seed), 12)
    q_latent = draw_q_latent(jax.random.fold_in(seeds[11], 71), 0)
    kv_latent = draw_kv_latent(jax.random.fold_in(seeds[11], 71), 0)
    w_value = bell_draw(seeds[2], (HEADS, LAT, VDIM), LAT ** -0.5, 0.25, ((0, 2),))
    w_out = bell_draw(seeds[3], (HEADS * VDIM, D), (HEADS * VDIM) ** -0.5, 0.125, ((0, 2),))
    resid = draw_resid(jax.random.fold_in(seeds[11], 71), 0)
    norm_gain = jnp.clip(1.0 + 0.18 * jax.random.normal(seeds[5], (D,), jnp.float32), 0.1, 1.9)
    w_gate = bell_draw(seeds[6], (EXPERTS, D, FF), D ** -0.5, 0.125, ((0, 16), (2, 2)))
    w_up = bell_draw(seeds[7], (EXPERTS, D, FF), D ** -0.5, 0.125, ((0, 16), (2, 2)))
    w_down_t = bell_draw(seeds[8], (EXPERTS, D, FF), FF ** -0.5, 0.15625, ((0, 16), (2, 2)))
    expert_ids_keys = jax.random.split(jax.random.fold_in(seeds[9], 1), L // ROWS)
    expert_ids_turns = jax.random.permutation(jax.random.fold_in(seeds[9], 3), L // ROWS)
    expert_ids = jax.vmap(lambda own, number: assign_block(jax.random.fold_in(seeds[9], 2), own, number, ROWS, EXPERTS, TOPK, CAP, 2))(expert_ids_keys, expert_ids_turns).reshape((L, TOPK))
    route_scores = jnp.clip(jnp.exp(math.log(1.0) - 2.3025851 * jax.random.uniform(seeds[10], (L, TOPK), jnp.float32) ** level_of(seeds[10], (L, TOPK), ((0, 32),), -0.2, 0.2)), 0.1, 1.0)
    return dict(q_latent=q_latent, kv_latent=kv_latent, w_value=w_value, w_out=w_out, resid=resid, norm_gain=norm_gain, w_gate=w_gate, w_up=w_up, w_down_t=w_down_t, expert_ids=expert_ids, route_scores=route_scores)


routed_factor = 2.446
norm_epsilon = 1e-06
masked_score = -1e+30

def attend_heads(q_latent, kv_latent, w_value, w_out):
    block_rows = 1024 if L % 1024 == 0 else L
    score_scale = (NOPE + ROPE) ** (-0.5)

    def one_head(inputs):
        head_queries, head_value = inputs
        pieces = []
        for block in range(L // block_rows):
            begin = block * block_rows
            finish = begin + block_rows
            latents = kv_latent[:finish]
            scores = jnp.dot(head_queries[begin:finish], latents.T, preferred_element_type=jnp.float32) * score_scale
            query_pos = begin + jnp.arange(block_rows, dtype=jnp.int32)
            key_pos = jnp.arange(finish, dtype=jnp.int32)
            visible = key_pos[None, :] <= query_pos[:, None]
            scores = jnp.where(visible, scores, masked_score)
            highest = lax.optimization_barrier(jnp.max(scores, axis=1, keepdims=True))
            exponent_terms = jnp.where(visible, jnp.exp(scores - highest), 0.0)
            denominator = lax.optimization_barrier(jnp.sum(exponent_terms, axis=1, keepdims=True))
            weighted = jnp.dot(exponent_terms.astype(jnp.bfloat16), latents[:, :LAT], preferred_element_type=jnp.float32)
            latent_out = (weighted / denominator).astype(jnp.bfloat16)
            pieces.append(jnp.dot(latent_out, head_value, preferred_element_type=jnp.float32).astype(jnp.bfloat16))
        return jnp.concatenate(pieces, axis=0)
    per_head = lax.map(one_head, (jnp.moveaxis(q_latent, 1, 0), w_value))
    flat_heads = jnp.moveaxis(per_head, 0, 1).reshape(L, HEADS * VDIM)
    return jnp.dot(flat_heads, w_out, preferred_element_type=jnp.float32)

def reference(q_latent, kv_latent, w_value, w_out, resid, norm_gain, w_gate, w_up, w_down_t, expert_ids, route_scores):
    attended = attend_heads(q_latent, kv_latent, w_value, w_out)
    after_attn = lax.optimization_barrier((resid.astype(jnp.float32) + attended).astype(jnp.bfloat16))
    widened = after_attn.astype(jnp.float32)
    mean_square = lax.optimization_barrier(jnp.mean(widened * widened, axis=1, keepdims=True))
    normed_flat = (widened * lax.rsqrt(mean_square + norm_epsilon) * norm_gain).astype(jnp.bfloat16)
    token_count = L
    blocks = token_count // ROWS
    per_block = ROWS * TOPK
    chosen = expert_ids.reshape(blocks, per_block)
    onehot = (chosen[:, :, None] == jnp.arange(EXPERTS, dtype=jnp.int32)[None, None, :]).astype(jnp.int32)
    ranking = lax.optimization_barrier(jnp.sum(onehot * (jnp.cumsum(onehot, axis=1) - 1), axis=2)).astype(jnp.int32)
    block_index = jnp.broadcast_to(jnp.arange(blocks, dtype=jnp.int32)[:, None], (blocks, per_block))
    entry_index = jnp.broadcast_to(jnp.arange(per_block, dtype=jnp.int32)[None, :], (blocks, per_block))
    owners = jnp.full((blocks, EXPERTS, CAP), -1, jnp.int32).at[block_index, chosen, ranking].set(entry_index)
    present = owners >= 0
    entries = jnp.where(present, owners, 0).astype(jnp.int32)
    block_column = jnp.arange(blocks, dtype=jnp.int32)[:, None, None]
    token_of = (block_column * ROWS + entries // TOPK).astype(jnp.int32)
    combine = route_scores / lax.optimization_barrier(jnp.sum(route_scores, axis=1, keepdims=True))
    combine_flat = combine.reshape(blocks * per_block)
    weight_of = jnp.where(present, combine_flat[block_column * per_block + entries], 0.0)
    token_major = jnp.transpose(token_of, (1, 0, 2)).reshape(EXPERTS, blocks * CAP)
    weight_major = jnp.transpose(weight_of, (1, 0, 2)).reshape(EXPERTS, blocks * CAP)

    def add_expert(accum, inputs):
        gate_weight, up_weight, down_weight, token_ids, token_weights = inputs
        rows_in = normed_flat[token_ids]
        gate = jnp.dot(rows_in, gate_weight, preferred_element_type=jnp.float32)
        upward = jnp.dot(rows_in, up_weight, preferred_element_type=jnp.float32)
        hidden = (jax.nn.silu(gate) * upward).astype(jnp.bfloat16)
        produced = jnp.dot(hidden, down_weight.T, preferred_element_type=jnp.float32).astype(jnp.bfloat16)
        accum = accum.at[token_ids].add(produced.astype(jnp.float32) * token_weights[:, None])
        return (accum, None)
    accum, unused = lax.scan(add_expert, jnp.zeros((token_count, D), jnp.float32), (w_gate, w_up, w_down_t, token_major, weight_major))
    return (widened + routed_factor * accum).astype(jnp.bfloat16)
```

```python
import functools
import math

import jax
import jax.numpy as jnp
from jax import lax
from jax.experimental import pallas as pl
from jax.experimental.pallas import tpu as pltpu
from jax.sharding import PartitionSpec as P

ROPE = 64
NOPE = 128
TOPK = 6

routed_factor = 2.446
norm_epsilon = 1e-06
masked_score = -1e30
LANES = 128
SQUARE = 4


def exp2_scale():
    return (NOPE + ROPE) ** (-0.5) * math.log2(math.e)


def attend_kernel(blocks, merge, first, last, mode_ref, q_ref, *refs):
    key_refs, refs = refs[:blocks], refs[blocks:]
    if not first:
        m_in, l_in, acc_in = refs[:3]
        refs = refs[3:]
    if last:
        wv_ref, out_ref = refs[:2]
        refs = refs[2:]
    m_s, l_s, acc_s, q_s, kt, kk, s0, s1, sems = refs
    heads, _, tokens = q_ref.shape
    units, _, columns = q_s.shape
    block_keys = key_refs[0].shape[1]
    latent = acc_s.shape[1]
    chunk = SQUARE * block_keys
    chunks = blocks // SQUARE
    visible = mode_ref[blocks + 1]
    total = visible * units
    factor = exp2_scale()
    lazy = chunks > 1 and units % 2 == 0

    def columns_of(i, n):
        return pl.ds(pl.multiple_of(i * n, LANES), n)

    def copy_of(i, source=None):
        return pltpu.make_async_copy(
            key_refs[0 if source is None else source], kt.at[:, columns_of(i, block_keys)], sems.at[i]
        )

    def wait_chunk(c):
        for j in range(SQUARE):
            copy_of(c * SQUARE + j).wait()

    def turn(i):
        kk[columns_of(i, block_keys), :] = jnp.transpose(kt[:, columns_of(i, block_keys)])

    for c in range(chunks):

        @pl.when(c < visible)
        def _():
            for j in range(SQUARE):
                copy_of(c * SQUARE + j, c * SQUARE + j).start()

    if first:
        m_s[...] = jnp.full(m_s.shape, masked_score, jnp.float32)
        l_s[...] = jnp.zeros(l_s.shape, jnp.float32)
        acc_s[...] = jnp.zeros(acc_s.shape, jnp.float32)
    else:
        m_s[...] = m_in[...]
        l_s[...] = l_in[...]
        acc_s[...] = acc_in[...]
    for h in range(heads):
        q_s[h // merge, :, (h % merge) * tokens : (h % merge + 1) * tokens] = q_ref[h]

    @pl.when(visible > 0)
    def _():
        wait_chunk(0)
        for i in range(SQUARE):
            turn(i)

    if not lazy:
        for c in range(1, chunks):

            @pl.when(c < visible)
            def _():
                wait_chunk(c)
                for i in range(SQUARE):
                    turn(c * SQUARE + i)

    def scores(t, buffer):
        t = jnp.maximum(jnp.minimum(t, total - 1), 0)
        buffer[...] = jnp.dot(
            kk[columns_of(t // units, chunk), :],
            q_s[t % units],
            preferred_element_type=jnp.float32,
        )

    def use(t, buffer):
        c, u = t // units, t % units
        if first:
            shape = (block_keys, columns)
            token = lax.broadcasted_iota(jnp.int32, shape, 1)
            gap = lax.broadcasted_iota(jnp.int32, shape, 0) - token % tokens
            s = jnp.concatenate(
                [
                    jnp.where(
                        gap <= mode_ref[c * SQUARE + j],
                        buffer[j * block_keys : (j + 1) * block_keys],
                        masked_score,
                    )
                    for j in range(SQUARE)
                ],
                axis=0,
            )
        else:
            s = buffer[...]
        old = m_s[u]
        new = jnp.maximum(old, jnp.max(s, axis=0, keepdims=True))
        alpha = jnp.exp2((old - new) * factor)
        p = jnp.exp2((s - new) * factor)
        l_s[u] = l_s[u] * alpha + jnp.sum(p, axis=0, keepdims=True)
        m_s[u] = new
        acc_s[u] = acc_s[u] * alpha + jnp.dot(
            kt[:latent, columns_of(c, chunk)],
            p.astype(jnp.bfloat16),
            preferred_element_type=jnp.float32,
        )

    scores(0, s0)

    def body(i, unused):
        t = 2 * i
        if lazy:

            @pl.when((t % units == 0) & (t // units + 1 < visible))
            def _():
                wait_chunk(t // units + 1)

        scores(t + 1, s1)
        use(t, s0)
        if lazy:
            each = -(-SQUARE * 2 // units)
            for j in range(each):
                place = jnp.minimum(t % units // 2 * each + j, SQUARE - 1)
                turn(jnp.minimum(t // units + 1, visible - 1) * SQUARE + place)
        scores(t + 2, s0)
        if units % 2 == 0:
            use(t + 1, s1)
        else:

            @pl.when(t + 1 < total)
            def _():
                use(t + 1, s1)

        return unused

    lax.fori_loop(0, (total + 1) // 2, body, 0)

    for h in range(heads if last else 0):
        u, span = h // merge, slice(h % merge * tokens, (h % merge + 1) * tokens)
        result = (acc_s[u][:, span] * (1.0 / l_s[u][:, span])).astype(jnp.bfloat16)
        out_ref[h] = lax.dot_general(
            wv_ref[h], result, (((0,), (0,)), ((), ())), preferred_element_type=jnp.float32
        ).astype(out_ref.dtype)


def attend(queries, key_blocks, mode, w_value, tokens, state=None, last=True):
    heads, depth, _ = queries.shape
    blocks, block_keys = len(key_blocks), key_blocks[0].shape[1]
    latent, value = w_value.shape[1:]
    merge = min(heads, max(1, 2 * LANES // tokens))
    units, columns = heads // merge, merge * tokens
    first = state is None

    def whole(*shape):
        return pl.BlockSpec(shape, lambda g, mode: (0,) * len(shape))

    states = [(units, 1, columns), (units, 1, columns), (units, latent, columns)]
    in_specs = [pl.BlockSpec((heads, depth, tokens), lambda g, mode: (0, 0, mode[blocks]))]
    in_specs += [pl.BlockSpec(memory_space=pl.ANY)] * blocks
    operands = [queries, *key_blocks]
    if not first:
        in_specs += [whole(*shape) for shape in states]
        operands += list(state)
    if last:
        in_specs.append(whole(heads, latent, value))
        operands.append(w_value)
        out_specs = whole(heads, value, tokens)
        out_shape = jax.ShapeDtypeStruct((heads, value, tokens), jnp.bfloat16)
    else:
        out_specs = [whole(*shape) for shape in states]
        out_shape = [jax.ShapeDtypeStruct(shape, jnp.float32) for shape in states]
    pairs = heads * tokens * blocks * block_keys
    made = pl.pallas_call(
        functools.partial(attend_kernel, blocks, merge, first, last),
        grid_spec=pltpu.PrefetchScalarGridSpec(
            num_scalar_prefetch=1,
            grid=(1,),
            in_specs=in_specs,
            out_specs=out_specs,
            scratch_shapes=([pltpu.VMEM(shape, jnp.float32) for shape in states] if last else [])
            + [
                pltpu.VMEM((units, depth, columns), jnp.bfloat16),
                pltpu.VMEM((depth, blocks * block_keys), jnp.bfloat16),
                pltpu.VMEM((blocks * block_keys, depth), jnp.bfloat16),
                pltpu.VMEM((SQUARE * block_keys, columns), jnp.float32),
                pltpu.VMEM((SQUARE * block_keys, columns), jnp.float32),
                pltpu.SemaphoreType.DMA((blocks,)),
            ],
        ),
        out_shape=out_shape,
        cost_estimate=pl.CostEstimate(
            flops=2 * pairs * (depth + latent),
            bytes_accessed=2 * blocks * block_keys * depth,
            transcendentals=pairs,
        ),
        compiler_params=pltpu.CompilerParams(vmem_limit_bytes=58 * 1024 * 1024),
    )(mode, *operands)
    return made.reshape(heads * value, tokens) if last else made


def expert_kernel(sources, batches, parts, slots, rank_ref, rank_t_ref, weight_ref, *refs):
    normed, refs = refs[: sources * batches], refs[sources * batches :]
    shards, refs = refs[: 3 * parts], refs[3 * parts :]
    kept, sent, row_buf, gate_buf, up_buf, down_buf, picked, total, row_sem, weight_sem = refs
    tokens = row_buf.shape[1]
    piece = tokens // batches
    bufs = (gate_buf, up_buf, down_buf)

    def row_copy(j, b):
        return pltpu.make_async_copy(
            normed[j * batches + b], row_buf.at[j, b * piece : (b + 1) * piece], row_sem.at[j, b]
        )

    def shard_copy(n):
        part, which = n // 3, n % 3
        return pltpu.make_async_copy(
            shards[n], bufs[which].at[part], weight_sem.at[part, which]
        )

    for j in range(sources):
        for b in range(batches):
            row_copy(j, b).start()
    early = 2
    for n in range(early):
        shard_copy(n).start()

    for j in range(sources):
        slot = lax.broadcasted_iota(jnp.int32, (slots, tokens), 0)
        place = (slot == rank_ref[j : j + 1, :]).astype(jnp.bfloat16)
        for b in range(batches):
            row_copy(j, b).wait()
        picked[j * slots : (j + 1) * slots, :] = jnp.dot(
            place, row_buf[j], preferred_element_type=jnp.float32
        ).astype(jnp.bfloat16)

    for n in range(early, 3 * parts):
        shard_copy(n).start()
    across = (((1,), (1,)), ((), ()))
    total[...] = jnp.zeros(total.shape, jnp.float32)

    def wait_for(part, which):
        pltpu.make_async_copy(
            shards[which], bufs[which].at[part], weight_sem.at[part, which]
        ).wait()

    def one_part(part, unused):
        rows = picked[...]
        wait_for(part, 0)
        gate = lax.dot_general(rows, gate_buf[part], across, preferred_element_type=jnp.float32)
        wait_for(part, 1)
        upward = lax.dot_general(rows, up_buf[part], across, preferred_element_type=jnp.float32)
        hidden = (gate / (1.0 + jnp.exp(-gate)) * upward).astype(jnp.bfloat16)
        wait_for(part, 2)
        total[...] += jnp.dot(hidden, down_buf[part], preferred_element_type=jnp.float32)
        return unused

    lax.fori_loop(0, parts, one_part, 0)

    for j in range(sources):
        slot = lax.broadcasted_iota(jnp.int32, (slots, tokens), 0)
        weight = jnp.sum(
            jnp.where(slot == rank_ref[j : j + 1, :], weight_ref[j : j + 1, :], 0.0),
            axis=1,
            keepdims=True,
        )
        scaled = (total[j * slots : (j + 1) * slots, :] * weight).astype(jnp.bfloat16)
        lane = lax.broadcasted_iota(jnp.int32, (tokens, slots), 1)
        back = (lane == rank_t_ref[:, j : j + 1]).astype(jnp.bfloat16)
        out_ref = kept if j < sources // 2 else sent
        out_ref[j % (sources // 2)] = jnp.dot(
            back, scaled, preferred_element_type=jnp.float32
        ).astype(jnp.bfloat16)


def experts(normed, shards, rank, weight, slots):
    sources, batches, parts = len(normed), len(normed[0]), len(shards)
    tokens = sum(piece.shape[0] for piece in normed[0])
    units, width = shards[0][0].shape
    flat = [array for shard in shards for array in shard]
    any_spec = pl.BlockSpec(memory_space=pl.ANY)
    vmem = pl.BlockSpec(memory_space=pltpu.VMEM)
    rows = sources * slots
    half = jax.ShapeDtypeStruct((sources // 2, tokens, width), jnp.bfloat16)
    return pl.pallas_call(
        functools.partial(expert_kernel, sources, batches, parts, slots),
        in_specs=[vmem] * 3 + [any_spec] * (sources * batches + len(flat)),
        out_specs=[vmem, vmem],
        out_shape=[half, half],
        scratch_shapes=[
            pltpu.VMEM((sources, tokens, width), jnp.bfloat16),
            pltpu.VMEM((parts, units, width), jnp.bfloat16),
            pltpu.VMEM((parts, units, width), jnp.bfloat16),
            pltpu.VMEM((parts, units, width), jnp.bfloat16),
            pltpu.VMEM((rows, width), jnp.bfloat16),
            pltpu.VMEM((rows, width), jnp.float32),
            pltpu.SemaphoreType.DMA((sources, batches)),
            pltpu.SemaphoreType.DMA((parts, 3)),
        ],
        cost_estimate=pl.CostEstimate(
            flops=6 * rows * width * units * parts,
            bytes_accessed=2 * (3 * parts * width * units + 2 * sources * tokens * width),
            transcendentals=rows * units * parts,
        ),
        compiler_params=pltpu.CompilerParams(vmem_limit_bytes=58 * 1024 * 1024),
    )(rank, rank.T, weight, *[piece for source in normed for piece in source], *flat)


def per_device(
    sizes,
    q_latent,
    kv_latent,
    w_value,
    w_out,
    resid,
    norm_gain,
    w_gate,
    w_up,
    w_down_t,
    expert_ids,
    route_scores,
):
    count, head_parts, group = sizes["ctx"], sizes["head"], sizes["head"] * sizes["ep"]
    tokens_here = q_latent.shape[0]
    rows, _ = resid.shape
    planes = count // SQUARE
    here = lax.axis_index("ctx")
    plane, spot = here // SQUARE, here % SQUARE

    def swap(value, bit):
        return lax.ppermute(value, "ctx", [(c, c ^ bit) for c in range(count)])

    def shift(value, by, wrap=True):
        pairs = []
        for c in range(count):
            to = c // SQUARE + by
            if wrap or 0 <= to < planes:
                pairs.append((c, to % planes * SQUARE + c % SQUARE))
        return lax.ppermute(value, "ctx", pairs)

    first = kv_latent.T
    key_blocks = []
    for by in range(planes):
        if by:
            first = shift(first, 1, wrap=False)
        across = swap(first, 2)
        beside = swap(first, 1)
        corner = swap(across, 1)
        key_blocks += [first, beside, across, corner]

    shards = [(w_gate[0].T, w_up[0].T, w_down_t[0].T)]
    for by in range(1, head_parts):
        pairs = [(i, (i + by) % head_parts) for i in range(head_parts)]
        shard = []
        for which in range(3):
            shard.append(lax.ppermute(shards[0][which], "head", pairs))
        shards.append(tuple(shard))

    combine = route_scores / jnp.sum(route_scores, axis=1, keepdims=True)
    table = jnp.concatenate([expert_ids.T.astype(jnp.float32), combine.T], axis=0)
    tables = lax.all_gather(table, "ctx", axis=0)

    queries = jnp.transpose(q_latent, (1, 2, 0))
    step = jnp.arange(SQUARE, dtype=jnp.int32)
    others = jnp.concatenate([(plane - by) * SQUARE + (spot ^ step) for by in range(planes)])
    far = jnp.int32(1 << 20)

    def mode_of(block, tokens, low, high):
        limit = jnp.where(others == here, block * tokens, jnp.where(others < here, far, -far))
        seen = jnp.clip(plane + 1 - low, 0, high - low)
        tail = jnp.stack([jnp.int32(block), seen])
        return jnp.concatenate([limit[low * SQUARE : high * SQUARE], tail]).astype(jnp.int32)

    def project(made):
        return lax.dot_general(
            made, w_out, (((0,), (0,)), ((), ())), preferred_element_type=jnp.float32
        )

    if group == 2 and rows % LANES == 0 and planes > 1:
        side = lax.axis_index("head") * sizes["ep"] + lax.axis_index("ep")
        halves = {"other": 1 - side, "own": side}
        near, distant = key_blocks[:SQUARE], key_blocks[SQUARE:]
        states = {
            which: attend(queries, near, mode_of(block, rows, 0, 1), w_value, rows, last=False)
            for which, block in halves.items()
        }

        def finish(which):
            mode = mode_of(halves[which], rows, 1, planes)
            return attend(queries, distant, mode, w_value, rows, states[which])

        partial = project(finish("other")).astype(jnp.bfloat16)
        came = lax.ppermute(partial, ("head", "ep"), [(0, 1), (1, 0)])
        attended = project(finish("own")) + came.astype(jnp.float32)
    else:
        made = [
            attend(queries, key_blocks, mode_of(b, LANES, 0, planes), w_value, LANES)
            for b in range(tokens_here // LANES)
        ]
        attended = lax.psum_scatter(
            project(jnp.concatenate(made, axis=1)),
            ("head", "ep"),
            scatter_dimension=0,
            tiled=True,
        )
    after_attn = lax.optimization_barrier(
        (resid.astype(jnp.float32) + attended).astype(jnp.bfloat16)
    )
    widened = after_attn.astype(jnp.float32)
    mean_square = jnp.mean(widened * widened, axis=1, keepdims=True)
    normed = (widened * lax.rsqrt(mean_square + norm_epsilon) * norm_gain).astype(jnp.bfloat16)

    arrived, first = [], normed
    for n in range(planes):
        if n:
            first = shift(first, 1)
        across = swap(first, 2)
        beside = swap(first, 1)
        corner = swap(across, 1)
        arrived.append([[first], [across], [beside], [corner]])

    capacity = 5 * rows * TOPK // (4 * count)
    slots = -(-capacity // 16) * 16
    named = tables[:, :TOPK, :] == here.astype(jnp.float32)
    chosen = jnp.any(named, axis=1)
    weight = jnp.sum(jnp.where(named, tables[:, TOPK:, :], 0.0), axis=1)
    before = jnp.arange(rows)[:, None] <= jnp.arange(rows)[None, :]
    ranking = jnp.dot(
        chosen.astype(jnp.bfloat16), before.astype(jnp.bfloat16), preferred_element_type=jnp.float32
    )
    rank = jnp.where(chosen, ranking - 1.0, -1.0).astype(jnp.int32)

    combined = None
    for n in range(planes):
        order = (plane - n) % planes * SQUARE + (spot ^ jnp.array([0, 2, 1, 3], jnp.int32))
        kept, sent = experts(arrived[n], shards, rank[order], weight[order], slots)
        other = swap(sent, 1)
        crossing = (kept[1].astype(jnp.float32) + other[1].astype(jnp.float32)).astype(jnp.bfloat16)
        crossing = swap(crossing, 2)
        summed = kept[0].astype(jnp.float32) + other[0].astype(jnp.float32) + crossing.astype(jnp.float32)
        if n:
            summed = shift(summed.astype(jnp.bfloat16), -n).astype(jnp.float32)
        combined = summed if combined is None else combined + summed
    return (widened + routed_factor * combined).astype(jnp.bfloat16)


def solution(mesh):
    placed = (
        P("ctx", ("head", "ep"), None),
        P("ctx", None),
        P(("head", "ep"), None, None),
        P(("head", "ep"), None),
        P(("ctx", "head", "ep"), None),
        P(),
        P("ctx", None, "head"),
        P("ctx", None, "head"),
        P("ctx", None, "head"),
        P(("ctx", "head", "ep"), None),
        P(("ctx", "head", "ep"), None),
    )

    def body(*arguments):
        return per_device(dict(mesh.shape), *arguments)

    return jax.shard_map(
        body,
        mesh=mesh,
        in_specs=placed,
        out_specs=P(("ctx", "head", "ep"), None),
        check_vma=False,
    )
```

```python
import functools
import math

import jax
import jax.numpy as jnp
from jax import lax
from jax.experimental import pallas as pl
from jax.experimental.pallas import tpu as pltpu
from jax.sharding import PartitionSpec as P

ROPE = 64
NOPE = 128
TOPK = 6

routed_factor = 2.446
norm_epsilon = 1e-06
masked_score = -1e30
LANES = 128
SQUARE = 4


def exp2_scale():
    return (NOPE + ROPE) ** (-0.5) * math.log2(math.e)


def attend_kernel(blocks, merge, given, last, mode_ref, q_ref, *refs):
    key_refs, refs = refs[:blocks], refs[blocks:]
    if given:
        states_in, refs = refs[: 3 * given], refs[3 * given :]
    if last:
        wv_ref, out_ref = refs[:2]
        refs = refs[2:]
    m_s, l_s, acc_s, q_s, kt, kk, s0, s1, sems = refs
    first = given == 0
    heads, _, tokens = q_ref.shape
    units, _, columns = q_s.shape
    block_keys = key_refs[0].shape[1]
    latent = acc_s.shape[1]
    chunk = SQUARE * block_keys
    chunks = blocks // SQUARE
    visible = mode_ref[blocks + 1]
    total = visible * units
    factor = exp2_scale()
    lazy = chunks > 1 and units % 2 == 0

    def columns_of(i, n):
        return pl.ds(pl.multiple_of(i * n, LANES), n)

    def copy_of(i, source=None):
        return pltpu.make_async_copy(
            key_refs[0 if source is None else source], kt.at[:, columns_of(i, block_keys)], sems.at[i]
        )

    def wait_chunk(c):
        for j in range(SQUARE):
            copy_of(c * SQUARE + j).wait()

    def turn(i):
        kk[columns_of(i, block_keys), :] = jnp.transpose(kt[:, columns_of(i, block_keys)])

    for c in range(chunks):

        @pl.when(c < visible)
        def _():
            for j in range(SQUARE):
                copy_of(c * SQUARE + j, c * SQUARE + j).start()

    if first:
        m_s[...] = jnp.full(m_s.shape, masked_score, jnp.float32)
        l_s[...] = jnp.zeros(l_s.shape, jnp.float32)
        acc_s[...] = jnp.zeros(acc_s.shape, jnp.float32)
    else:
        each = units // given
        for g in range(given):
            for ref, source in zip((m_s, l_s, acc_s), states_in[3 * g : 3 * g + 3]):
                ref[g * each : (g + 1) * each] = source[...]
    for h in range(heads):
        q_s[h // merge, :, (h % merge) * tokens : (h % merge + 1) * tokens] = q_ref[h]

    @pl.when(visible > 0)
    def _():
        wait_chunk(0)
        for i in range(SQUARE):
            turn(i)

    if not lazy:
        for c in range(1, chunks):

            @pl.when(c < visible)
            def _():
                wait_chunk(c)
                for i in range(SQUARE):
                    turn(c * SQUARE + i)

    def scores(t, buffer):
        t = jnp.maximum(jnp.minimum(t, total - 1), 0)
        buffer[...] = jnp.dot(
            kk[columns_of(t // units, chunk), :],
            q_s[t % units],
            preferred_element_type=jnp.float32,
        )

    def use(t, buffer):
        c, u = t // units, t % units
        if first:
            shape = (block_keys, columns)
            token = lax.broadcasted_iota(jnp.int32, shape, 1)
            gap = lax.broadcasted_iota(jnp.int32, shape, 0) - token % tokens
            s = jnp.concatenate(
                [
                    jnp.where(
                        gap <= mode_ref[c * SQUARE + j],
                        buffer[j * block_keys : (j + 1) * block_keys],
                        masked_score,
                    )
                    for j in range(SQUARE)
                ],
                axis=0,
            )
        else:
            s = buffer[...]
        old = m_s[u]
        new = jnp.maximum(old, jnp.max(s, axis=0, keepdims=True))
        alpha = jnp.exp2((old - new) * factor)
        p = jnp.exp2((s - new) * factor)
        l_s[u] = l_s[u] * alpha + jnp.sum(p, axis=0, keepdims=True)
        m_s[u] = new
        acc_s[u] = acc_s[u] * alpha + jnp.dot(
            kt[:latent, columns_of(c, chunk)],
            p.astype(jnp.bfloat16),
            preferred_element_type=jnp.float32,
        )

    scores(0, s0)

    def body(i, unused):
        t = 2 * i
        if lazy:

            @pl.when((t % units == 0) & (t // units + 1 < visible))
            def _():
                wait_chunk(t // units + 1)

        scores(t + 1, s1)
        use(t, s0)
        if lazy:
            each = -(-SQUARE * 2 // units)
            for j in range(each):
                place = jnp.minimum(t % units // 2 * each + j, SQUARE - 1)
                turn(jnp.minimum(t // units + 1, visible - 1) * SQUARE + place)
        scores(t + 2, s0)
        if units % 2 == 0:
            use(t + 1, s1)
        else:

            @pl.when(t + 1 < total)
            def _():
                use(t + 1, s1)

        return unused

    lax.fori_loop(0, (total + 1) // 2, body, 0)

    for h in range(heads if last else 0):
        u, span = h // merge, slice(h % merge * tokens, (h % merge + 1) * tokens)
        result = (acc_s[u][:, span] * (1.0 / l_s[u][:, span])).astype(jnp.bfloat16)
        out_ref[h] = lax.dot_general(
            wv_ref[h], result, (((0,), (0,)), ((), ())), preferred_element_type=jnp.float32
        ).astype(out_ref.dtype)


def attend(queries, key_blocks, mode, w_value, tokens, given=(), last=True, part=0, parts=1):
    heads, depth, _ = queries.shape
    heads = heads // parts
    blocks, block_keys = len(key_blocks), key_blocks[0].shape[1]
    latent, value = w_value.shape[1:]
    merge = min(heads, max(1, 2 * LANES // tokens))
    units, columns = heads // merge, merge * tokens

    def whole(*shape):
        return pl.BlockSpec(shape, lambda g, mode: (0,) * len(shape))

    states = [(units, 1, columns), (units, 1, columns), (units, latent, columns)]
    in_specs = [pl.BlockSpec((heads, depth, tokens), lambda g, mode: (part, 0, mode[blocks]))]
    in_specs += [pl.BlockSpec(memory_space=pl.ANY)] * blocks
    operands = [queries, *key_blocks]
    for state in given:
        in_specs += [whole(units // len(given), *shape[1:]) for shape in states]
        operands += list(state)
    if last:
        in_specs.append(whole(heads, latent, value))
        operands.append(w_value)
        out_specs = whole(heads, value, tokens)
        out_shape = jax.ShapeDtypeStruct((heads, value, tokens), jnp.bfloat16)
    else:
        out_specs = [whole(*shape) for shape in states]
        out_shape = [jax.ShapeDtypeStruct(shape, jnp.float32) for shape in states]
    pairs = heads * tokens * blocks * block_keys
    made = pl.pallas_call(
        functools.partial(attend_kernel, blocks, merge, len(given), last),
        grid_spec=pltpu.PrefetchScalarGridSpec(
            num_scalar_prefetch=1,
            grid=(1,),
            in_specs=in_specs,
            out_specs=out_specs,
            scratch_shapes=([pltpu.VMEM(shape, jnp.float32) for shape in states] if last else [])
            + [
                pltpu.VMEM((units, depth, columns), jnp.bfloat16),
                pltpu.VMEM((depth, blocks * block_keys), jnp.bfloat16),
                pltpu.VMEM((blocks * block_keys, depth), jnp.bfloat16),
                pltpu.VMEM((SQUARE * block_keys, columns), jnp.float32),
                pltpu.VMEM((SQUARE * block_keys, columns), jnp.float32),
                pltpu.SemaphoreType.DMA((blocks,)),
            ],
        ),
        out_shape=out_shape,
        cost_estimate=pl.CostEstimate(
            flops=2 * pairs * (depth + latent),
            bytes_accessed=2 * blocks * block_keys * depth,
            transcendentals=pairs,
        ),
        compiler_params=pltpu.CompilerParams(vmem_limit_bytes=58 * 1024 * 1024),
    )(mode, *operands)
    return made.reshape(heads * value, tokens) if last else made


def expert_kernel(sources, batches, parts, slots, rank_ref, rank_t_ref, weight_ref, *refs):
    normed, refs = refs[: sources * batches], refs[sources * batches :]
    shards, refs = refs[: 3 * parts], refs[3 * parts :]
    kept, sent, row_buf, gate_buf, up_buf, down_buf, picked, total, row_sem, weight_sem = refs
    tokens = row_buf.shape[1]
    piece = tokens // batches
    bufs = (gate_buf, up_buf, down_buf)

    def row_copy(j, b):
        return pltpu.make_async_copy(
            normed[j * batches + b], row_buf.at[j, b * piece : (b + 1) * piece], row_sem.at[j, b]
        )

    def shard_copy(n):
        part, which = n // 3, n % 3
        return pltpu.make_async_copy(
            shards[n], bufs[which].at[part], weight_sem.at[part, which]
        )

    for j in range(sources):
        for b in range(batches):
            row_copy(j, b).start()
    early = 2
    for n in range(early):
        shard_copy(n).start()

    for j in range(sources):
        slot = lax.broadcasted_iota(jnp.int32, (slots, tokens), 0)
        place = (slot == rank_ref[j : j + 1, :]).astype(jnp.bfloat16)
        for b in range(batches):
            row_copy(j, b).wait()
        picked[j * slots : (j + 1) * slots, :] = jnp.dot(
            place, row_buf[j], preferred_element_type=jnp.float32
        ).astype(jnp.bfloat16)

    for n in range(early, 3 * parts):
        shard_copy(n).start()
    across = (((1,), (1,)), ((), ()))
    total[...] = jnp.zeros(total.shape, jnp.float32)

    def wait_for(part, which):
        pltpu.make_async_copy(
            shards[which], bufs[which].at[part], weight_sem.at[part, which]
        ).wait()

    def one_part(part, unused):
        rows = picked[...]
        wait_for(part, 0)
        gate = lax.dot_general(rows, gate_buf[part], across, preferred_element_type=jnp.float32)
        wait_for(part, 1)
        upward = lax.dot_general(rows, up_buf[part], across, preferred_element_type=jnp.float32)
        hidden = (gate / (1.0 + jnp.exp(-gate)) * upward).astype(jnp.bfloat16)
        wait_for(part, 2)
        total[...] += jnp.dot(hidden, down_buf[part], preferred_element_type=jnp.float32)
        return unused

    lax.fori_loop(0, parts, one_part, 0)

    for j in range(sources):
        slot = lax.broadcasted_iota(jnp.int32, (slots, tokens), 0)
        weight = jnp.sum(
            jnp.where(slot == rank_ref[j : j + 1, :], weight_ref[j : j + 1, :], 0.0),
            axis=1,
            keepdims=True,
        )
        scaled = (total[j * slots : (j + 1) * slots, :] * weight).astype(jnp.bfloat16)
        lane = lax.broadcasted_iota(jnp.int32, (tokens, slots), 1)
        back = (lane == rank_t_ref[:, j : j + 1]).astype(jnp.bfloat16)
        out_ref = kept if j < sources // 2 else sent
        out_ref[j % (sources // 2)] = jnp.dot(
            back, scaled, preferred_element_type=jnp.float32
        ).astype(jnp.bfloat16)


def experts(normed, shards, rank, weight, slots):
    sources, batches, parts = len(normed), len(normed[0]), len(shards)
    tokens = sum(piece.shape[0] for piece in normed[0])
    units, width = shards[0][0].shape
    flat = [array for shard in shards for array in shard]
    any_spec = pl.BlockSpec(memory_space=pl.ANY)
    vmem = pl.BlockSpec(memory_space=pltpu.VMEM)
    rows = sources * slots
    half = jax.ShapeDtypeStruct((sources // 2, tokens, width), jnp.bfloat16)
    return pl.pallas_call(
        functools.partial(expert_kernel, sources, batches, parts, slots),
        in_specs=[vmem] * 3 + [any_spec] * (sources * batches + len(flat)),
        out_specs=[vmem, vmem],
        out_shape=[half, half],
        scratch_shapes=[
            pltpu.VMEM((sources, tokens, width), jnp.bfloat16),
            pltpu.VMEM((parts, units, width), jnp.bfloat16),
            pltpu.VMEM((parts, units, width), jnp.bfloat16),
            pltpu.VMEM((parts, units, width), jnp.bfloat16),
            pltpu.VMEM((rows, width), jnp.bfloat16),
            pltpu.VMEM((rows, width), jnp.float32),
            pltpu.SemaphoreType.DMA((sources, batches)),
            pltpu.SemaphoreType.DMA((parts, 3)),
        ],
        cost_estimate=pl.CostEstimate(
            flops=6 * rows * width * units * parts,
            bytes_accessed=2 * (3 * parts * width * units + 2 * sources * tokens * width),
            transcendentals=rows * units * parts,
        ),
        compiler_params=pltpu.CompilerParams(vmem_limit_bytes=58 * 1024 * 1024),
    )(rank, rank.T, weight, *[piece for source in normed for piece in source], *flat)


def per_device(
    sizes,
    q_latent,
    kv_latent,
    w_value,
    w_out,
    resid,
    norm_gain,
    w_gate,
    w_up,
    w_down_t,
    expert_ids,
    route_scores,
):
    count, head_parts, group = sizes["ctx"], sizes["head"], sizes["head"] * sizes["ep"]
    tokens_here, heads_here = q_latent.shape[:2]
    rows, _ = resid.shape
    planes = count // SQUARE
    here = lax.axis_index("ctx")
    plane, spot = here // SQUARE, here % SQUARE

    def swap(value, bit):
        return lax.ppermute(value, "ctx", [(c, c ^ bit) for c in range(count)])

    def shift(value, by, wrap=True):
        pairs = []
        for c in range(count):
            to = c // SQUARE + by
            if wrap or 0 <= to < planes:
                pairs.append((c, to % planes * SQUARE + c % SQUARE))
        return lax.ppermute(value, "ctx", pairs)

    first = kv_latent.T
    key_blocks = []
    for by in range(planes):
        if by:
            first = shift(first, 1, wrap=False)
        across = swap(first, 2)
        beside = swap(first, 1)
        corner = swap(across, 1)
        key_blocks += [first, beside, across, corner]

    shards = [(w_gate[0].T, w_up[0].T, w_down_t[0].T)]
    for by in range(1, head_parts):
        pairs = [(i, (i + by) % head_parts) for i in range(head_parts)]
        shard = []
        for which in range(3):
            shard.append(lax.ppermute(shards[0][which], "head", pairs))
        shards.append(tuple(shard))

    combine = route_scores / jnp.sum(route_scores, axis=1, keepdims=True)
    named = expert_ids.T[None] == jnp.arange(count, dtype=jnp.int32)[:, None, None]
    chosen = jnp.any(named, axis=1)
    before = jnp.arange(rows)[:, None] <= jnp.arange(rows)[None, :]
    ranking = jnp.dot(
        chosen.astype(jnp.bfloat16), before.astype(jnp.bfloat16), preferred_element_type=jnp.float32
    )
    table = jnp.stack(
        [
            jnp.where(chosen, ranking - 1.0, -1.0),
            jnp.sum(jnp.where(named, combine.T[None], 0.0), axis=1),
        ],
        axis=1,
    )
    tables = lax.all_to_all(table, "ctx", split_axis=0, concat_axis=0, tiled=True)

    queries = jnp.transpose(q_latent, (1, 2, 0))
    step = jnp.arange(SQUARE, dtype=jnp.int32)
    others = jnp.concatenate([(plane - by) * SQUARE + (spot ^ step) for by in range(planes)])
    far = jnp.int32(1 << 20)

    def mode_of(block, tokens, low, high):
        limit = jnp.where(others == here, block * tokens, jnp.where(others < here, far, -far))
        seen = jnp.clip(plane + 1 - low, 0, high - low)
        tail = jnp.stack([jnp.int32(block), seen])
        return jnp.concatenate([limit[low * SQUARE : high * SQUARE], tail]).astype(jnp.int32)

    def project(made):
        return lax.dot_general(
            made, w_out, (((0,), (0,)), ((), ())), preferred_element_type=jnp.float32
        )

    if group == 2 and rows % LANES == 0 and planes > 1:
        side = lax.axis_index("head") * sizes["ep"] + lax.axis_index("ep")
        halves = {"other": 1 - side, "own": side}
        near, distant = key_blocks[:SQUARE], key_blocks[SQUARE:]
        cuts = {"other": 2 if heads_here % 4 == 0 else 1, "own": 1}
        states = {
            which: [
                attend(
                    queries, near, mode_of(block, rows, 0, 1), w_value, rows, last=False, part=part, parts=cuts[which]
                )
                for part in range(cuts[which])
            ]
            for which, block in halves.items()
        }

        def finish(which):
            mode = mode_of(halves[which], rows, 1, planes)
            return attend(queries, distant, mode, w_value, rows, states[which])

        partial = project(finish("other")).astype(jnp.bfloat16)
        came = lax.ppermute(partial, ("head", "ep"), [(0, 1), (1, 0)])
        attended = project(finish("own")) + came.astype(jnp.float32)
    else:
        made = [
            attend(queries, key_blocks, mode_of(b, LANES, 0, planes), w_value, LANES)
            for b in range(tokens_here // LANES)
        ]
        attended = lax.psum_scatter(
            project(jnp.concatenate(made, axis=1)),
            ("head", "ep"),
            scatter_dimension=0,
            tiled=True,
        )
    after_attn = lax.optimization_barrier(
        (resid.astype(jnp.float32) + attended).astype(jnp.bfloat16)
    )
    widened = after_attn.astype(jnp.float32)
    mean_square = jnp.mean(widened * widened, axis=1, keepdims=True)
    normed = (widened * lax.rsqrt(mean_square + norm_epsilon) * norm_gain).astype(jnp.bfloat16)

    arrived, first = [], normed
    for n in range(planes):
        if n:
            first = shift(first, 1)
        across = swap(first, 2)
        beside = swap(first, 1)
        corner = swap(across, 1)
        arrived.append([[first], [across], [beside], [corner]])

    capacity = 5 * rows * TOPK // (4 * count)
    slots = -(-capacity // 16) * 16
    rank = tables[:, 0].astype(jnp.int32)
    weight = tables[:, 1]

    carried = summed = None
    for n in list(range(1, planes)) + [0]:
        order = (plane - n) % planes * SQUARE + (spot ^ jnp.array([0, 2, 1, 3], jnp.int32))
        kept, sent = experts(arrived[n], shards, rank[order], weight[order], slots)
        other = swap(sent, 1)
        crossing = (kept[1].astype(jnp.float32) + other[1].astype(jnp.float32)).astype(jnp.bfloat16)
        crossing = swap(crossing, 2)
        summed = kept[0].astype(jnp.float32) + other[0].astype(jnp.float32) + crossing.astype(jnp.float32)
        if carried is not None:
            summed = summed + carried.astype(jnp.float32)
        if n:
            carried = shift(summed.astype(jnp.bfloat16), 1)
    return (widened + routed_factor * summed).astype(jnp.bfloat16)


def solution(mesh):
    placed = (
        P("ctx", ("head", "ep"), None),
        P("ctx", None),
        P(("head", "ep"), None, None),
        P(("head", "ep"), None),
        P(("ctx", "head", "ep"), None),
        P(),
        P("ctx", None, "head"),
        P("ctx", None, "head"),
        P("ctx", None, "head"),
        P(("ctx", "head", "ep"), None),
        P(("ctx", "head", "ep"), None),
    )

    def body(*arguments):
        return per_device(dict(mesh.shape), *arguments)

    return jax.shard_map(
        body,
        mesh=mesh,
        in_specs=placed,
        out_specs=P(("ctx", "head", "ep"), None),
        check_vma=False,
    )
```

```python
import functools
import math

import jax
import jax.numpy as jnp
from jax import lax
from jax.experimental import pallas as pl
from jax.experimental.pallas import tpu as pltpu
from jax.sharding import PartitionSpec as P

ROPE = 64
NOPE = 128
TOPK = 6

routed_factor = 2.446
norm_epsilon = 1e-06
masked_score = -1e30
LANES = 128
SQUARE = 4


def exp2_scale():
    return (NOPE + ROPE) ** (-0.5) * math.log2(math.e)


def attend_kernel(blocks, merge, given, last, mode_ref, q_ref, *refs):
    key_refs, refs = refs[:blocks], refs[blocks:]
    if given:
        states_in, refs = refs[: 3 * given], refs[3 * given :]
    if last:
        wv_ref, out_ref = refs[:2]
        refs = refs[2:]
    m_s, l_s, acc_s, q_s, kt, kk, s0, s1, sems = refs
    first = given == 0
    heads, _, tokens = q_ref.shape
    units, _, columns = q_s.shape
    block_keys = key_refs[0].shape[1]
    latent = acc_s.shape[1]
    chunk = SQUARE * block_keys
    chunks = blocks // SQUARE
    visible = mode_ref[blocks + 1]
    total = visible * units
    factor = exp2_scale()
    lazy = chunks > 1 and units % 2 == 0

    def columns_of(i, n):
        return pl.ds(pl.multiple_of(i * n, LANES), n)

    def copy_of(i, source=None):
        return pltpu.make_async_copy(
            key_refs[0 if source is None else source], kt.at[:, columns_of(i, block_keys)], sems.at[i]
        )

    def wait_chunk(c):
        for j in range(SQUARE):
            copy_of(c * SQUARE + j).wait()

    def turn(i):
        kk[columns_of(i, block_keys), :] = jnp.transpose(kt[:, columns_of(i, block_keys)])

    for c in range(chunks):

        @pl.when(c < visible)
        def _():
            for j in range(SQUARE):
                copy_of(c * SQUARE + j, c * SQUARE + j).start()

    if first:
        m_s[...] = jnp.full(m_s.shape, masked_score, jnp.float32)
        l_s[...] = jnp.zeros(l_s.shape, jnp.float32)
        acc_s[...] = jnp.zeros(acc_s.shape, jnp.float32)
    else:
        each = units // given
        for g in range(given):
            for ref, source in zip((m_s, l_s, acc_s), states_in[3 * g : 3 * g + 3]):
                ref[g * each : (g + 1) * each] = source[...]
    for h in range(heads):
        q_s[h // merge, :, (h % merge) * tokens : (h % merge + 1) * tokens] = q_ref[h]

    @pl.when(visible > 0)
    def _():
        wait_chunk(0)
        for i in range(SQUARE):
            turn(i)

    if not lazy:
        for c in range(1, chunks):

            @pl.when(c < visible)
            def _():
                wait_chunk(c)
                for i in range(SQUARE):
                    turn(c * SQUARE + i)

    def scores(t, buffer):
        t = jnp.maximum(jnp.minimum(t, total - 1), 0)
        buffer[...] = jnp.dot(
            kk[columns_of(t // units, chunk), :],
            q_s[t % units],
            preferred_element_type=jnp.float32,
        )

    def use(t, buffer):
        c, u = t // units, t % units
        if first:
            shape = (block_keys, columns)
            token = lax.broadcasted_iota(jnp.int32, shape, 1)
            gap = lax.broadcasted_iota(jnp.int32, shape, 0) - token % tokens
            s = jnp.concatenate(
                [
                    jnp.where(
                        gap <= mode_ref[c * SQUARE + j],
                        buffer[j * block_keys : (j + 1) * block_keys],
                        masked_score,
                    )
                    for j in range(SQUARE)
                ],
                axis=0,
            )
        else:
            s = buffer[...]
        old = m_s[u]
        new = jnp.maximum(old, jnp.max(s, axis=0, keepdims=True))
        alpha = jnp.exp2((old - new) * factor)
        p = jnp.exp2((s - new) * factor)
        l_s[u] = l_s[u] * alpha + jnp.sum(p, axis=0, keepdims=True)
        m_s[u] = new
        acc_s[u] = acc_s[u] * alpha + jnp.dot(
            kt[:latent, columns_of(c, chunk)],
            p.astype(jnp.bfloat16),
            preferred_element_type=jnp.float32,
        )

    scores(0, s0)

    def body(i, unused):
        t = 2 * i
        if lazy:

            @pl.when((t % units == 0) & (t // units + 1 < visible))
            def _():
                wait_chunk(t // units + 1)

        scores(t + 1, s1)
        use(t, s0)
        if lazy:
            each = -(-SQUARE * 2 // units)
            for j in range(each):
                place = jnp.minimum(t % units // 2 * each + j, SQUARE - 1)
                turn(jnp.minimum(t // units + 1, visible - 1) * SQUARE + place)
        scores(t + 2, s0)
        if units % 2 == 0:
            use(t + 1, s1)
        else:

            @pl.when(t + 1 < total)
            def _():
                use(t + 1, s1)

        return unused

    lax.fori_loop(0, (total + 1) // 2, body, 0)

    for h in range(heads if last else 0):
        u, span = h // merge, slice(h % merge * tokens, (h % merge + 1) * tokens)
        result = (acc_s[u][:, span] * (1.0 / l_s[u][:, span])).astype(jnp.bfloat16)
        out_ref[h] = lax.dot_general(
            wv_ref[h], result, (((0,), (0,)), ((), ())), preferred_element_type=jnp.float32
        ).astype(out_ref.dtype)


def attend(queries, key_blocks, mode, w_value, tokens, given=(), last=True, part=0, parts=1):
    heads, depth, _ = queries.shape
    heads = heads // parts
    blocks, block_keys = len(key_blocks), key_blocks[0].shape[1]
    latent, value = w_value.shape[1:]
    merge = min(heads, max(1, 2 * LANES // tokens))
    units, columns = heads // merge, merge * tokens

    def whole(*shape):
        return pl.BlockSpec(shape, lambda g, mode: (0,) * len(shape))

    states = [(units, 1, columns), (units, 1, columns), (units, latent, columns)]
    in_specs = [pl.BlockSpec((heads, depth, tokens), lambda g, mode: (part, 0, mode[blocks]))]
    in_specs += [pl.BlockSpec(memory_space=pl.ANY)] * blocks
    operands = [queries, *key_blocks]
    for state in given:
        in_specs += [whole(units // len(given), *shape[1:]) for shape in states]
        operands += list(state)
    if last:
        in_specs.append(whole(heads, latent, value))
        operands.append(w_value)
        out_specs = whole(heads, value, tokens)
        out_shape = jax.ShapeDtypeStruct((heads, value, tokens), jnp.bfloat16)
    else:
        out_specs = [whole(*shape) for shape in states]
        out_shape = [jax.ShapeDtypeStruct(shape, jnp.float32) for shape in states]
    pairs = heads * tokens * blocks * block_keys
    made = pl.pallas_call(
        functools.partial(attend_kernel, blocks, merge, len(given), last),
        grid_spec=pltpu.PrefetchScalarGridSpec(
            num_scalar_prefetch=1,
            grid=(1,),
            in_specs=in_specs,
            out_specs=out_specs,
            scratch_shapes=([pltpu.VMEM(shape, jnp.float32) for shape in states] if last else [])
            + [
                pltpu.VMEM((units, depth, columns), jnp.bfloat16),
                pltpu.VMEM((depth, blocks * block_keys), jnp.bfloat16),
                pltpu.VMEM((blocks * block_keys, depth), jnp.bfloat16),
                pltpu.VMEM((SQUARE * block_keys, columns), jnp.float32),
                pltpu.VMEM((SQUARE * block_keys, columns), jnp.float32),
                pltpu.SemaphoreType.DMA((blocks,)),
            ],
        ),
        out_shape=out_shape,
        cost_estimate=pl.CostEstimate(
            flops=2 * pairs * (depth + latent),
            bytes_accessed=2 * blocks * block_keys * depth,
            transcendentals=pairs,
        ),
        compiler_params=pltpu.CompilerParams(vmem_limit_bytes=58 * 1024 * 1024),
    )(mode, *operands)
    return made.reshape(heads * value, tokens) if last else made


def expert_kernel(sources, batches, parts, slots, rank_ref, rank_t_ref, weight_ref, *refs):
    normed, refs = refs[: sources * batches], refs[sources * batches :]
    shards, refs = refs[: 3 * parts], refs[3 * parts :]
    kept, sent, row_buf, in_buf, down_buf, picked, made_buf, total, row_sem, weight_sem = refs
    tokens = row_buf.shape[1]
    piece = tokens // batches

    def row_copy(j, b):
        return pltpu.make_async_copy(
            normed[j * batches + b], row_buf.at[j, b * piece : (b + 1) * piece], row_sem.at[j, b]
        )

    def shard_copy(n):
        part, which = n // 3, n % 3
        place = in_buf.at[part, which] if which < 2 else down_buf.at[part]
        return pltpu.make_async_copy(shards[n], place, weight_sem.at[part, which])

    for j in range(sources):
        for b in range(batches):
            row_copy(j, b).start()
    for j in range(sources):
        slot = lax.broadcasted_iota(jnp.int32, (slots, tokens), 0)
        place = (slot == rank_ref[j : j + 1, :]).astype(jnp.bfloat16)
        for b in range(batches):
            row_copy(j, b).wait()
        if 0 < j <= 3:
            shard_copy(j - 1).start()
        picked[j * slots : (j + 1) * slots, :] = jnp.dot(
            place, row_buf[j], preferred_element_type=jnp.float32
        ).astype(jnp.bfloat16)

    for n in range(min(3, sources - 1), 3 * parts):
        shard_copy(n).start()
    across = (((1,), (1,)), ((), ()))
    total[...] = jnp.zeros(total.shape, jnp.float32)

    def one_part(part, unused):
        def one_input(which, inner):
            pltpu.make_async_copy(
                shards[0], in_buf.at[part, which], weight_sem.at[part, which]
            ).wait()
            made_buf[which] = lax.dot_general(
                picked[...], in_buf[part, which], across, preferred_element_type=jnp.float32
            )
            return inner

        lax.fori_loop(0, 2, one_input, 0)
        gate = made_buf[0]
        hidden = (gate / (1.0 + jnp.exp(-gate)) * made_buf[1]).astype(jnp.bfloat16)
        pltpu.make_async_copy(shards[2], down_buf.at[part], weight_sem.at[part, 2]).wait()
        total[...] += jnp.dot(hidden, down_buf[part], preferred_element_type=jnp.float32)
        return unused

    lax.fori_loop(0, parts, one_part, 0)

    for j in range(sources):
        slot = lax.broadcasted_iota(jnp.int32, (slots, tokens), 0)
        weight = jnp.sum(
            jnp.where(slot == rank_ref[j : j + 1, :], weight_ref[j : j + 1, :], 0.0),
            axis=1,
            keepdims=True,
        )
        scaled = (total[j * slots : (j + 1) * slots, :] * weight).astype(jnp.bfloat16)
        lane = lax.broadcasted_iota(jnp.int32, (tokens, slots), 1)
        back = (lane == rank_t_ref[:, j : j + 1]).astype(jnp.bfloat16)
        out_ref = kept if j < sources // 2 else sent
        out_ref[j % (sources // 2)] = jnp.dot(
            back, scaled, preferred_element_type=jnp.float32
        ).astype(jnp.bfloat16)


def experts(normed, shards, rank, weight, slots):
    sources, batches, parts = len(normed), len(normed[0]), len(shards)
    tokens = sum(piece.shape[0] for piece in normed[0])
    units, width = shards[0][0].shape
    flat = [array for shard in shards for array in shard]
    any_spec = pl.BlockSpec(memory_space=pl.ANY)
    vmem = pl.BlockSpec(memory_space=pltpu.VMEM)
    rows = sources * slots
    half = jax.ShapeDtypeStruct((sources // 2, tokens, width), jnp.bfloat16)
    return pl.pallas_call(
        functools.partial(expert_kernel, sources, batches, parts, slots),
        in_specs=[vmem] * 3 + [any_spec] * (sources * batches + len(flat)),
        out_specs=[vmem, vmem],
        out_shape=[half, half],
        scratch_shapes=[
            pltpu.VMEM((sources, tokens, width), jnp.bfloat16),
            pltpu.VMEM((parts, 2, units, width), jnp.bfloat16),
            pltpu.VMEM((parts, units, width), jnp.bfloat16),
            pltpu.VMEM((rows, width), jnp.bfloat16),
            pltpu.VMEM((2, rows, units), jnp.float32),
            pltpu.VMEM((rows, width), jnp.float32),
            pltpu.SemaphoreType.DMA((sources, batches)),
            pltpu.SemaphoreType.DMA((parts, 3)),
        ],
        cost_estimate=pl.CostEstimate(
            flops=6 * rows * width * units * parts,
            bytes_accessed=2 * (3 * parts * width * units + 2 * sources * tokens * width),
            transcendentals=rows * units * parts,
        ),
        compiler_params=pltpu.CompilerParams(vmem_limit_bytes=58 * 1024 * 1024),
    )(rank, rank.T, weight, *[piece for source in normed for piece in source], *flat)


def per_device(
    sizes,
    q_latent,
    kv_latent,
    w_value,
    w_out,
    resid,
    norm_gain,
    w_gate,
    w_up,
    w_down_t,
    expert_ids,
    route_scores,
):
    count, head_parts, group = sizes["ctx"], sizes["head"], sizes["head"] * sizes["ep"]
    tokens_here, heads_here = q_latent.shape[:2]
    rows, _ = resid.shape
    planes = count // SQUARE
    here = lax.axis_index("ctx")
    plane, spot = here // SQUARE, here % SQUARE

    def swap(value, bit):
        return lax.ppermute(value, "ctx", [(c, c ^ bit) for c in range(count)])

    def shift(value, by, wrap=True):
        pairs = []
        for c in range(count):
            to = c // SQUARE + by
            if wrap or 0 <= to < planes:
                pairs.append((c, to % planes * SQUARE + c % SQUARE))
        return lax.ppermute(value, "ctx", pairs)

    first = kv_latent.T
    key_blocks = []
    for by in range(planes):
        if by:
            first = shift(first, 1, wrap=False)
        across = swap(first, 2)
        beside = swap(first, 1)
        corner = swap(across, 1)
        key_blocks += [first, beside, across, corner]

    shards = [(w_gate[0].T, w_up[0].T, w_down_t[0].T)]
    for by in range(1, head_parts):
        pairs = [(i, (i + by) % head_parts) for i in range(head_parts)]
        shard = []
        for which in range(3):
            shard.append(lax.ppermute(shards[0][which], "head", pairs))
        shards.append(tuple(shard))

    combine = route_scores / jnp.sum(route_scores, axis=1, keepdims=True)
    named = expert_ids.T[None] == jnp.arange(count, dtype=jnp.int32)[:, None, None]
    chosen = jnp.any(named, axis=1)
    before = jnp.arange(rows)[:, None] <= jnp.arange(rows)[None, :]
    ranking = jnp.dot(
        chosen.astype(jnp.bfloat16), before.astype(jnp.bfloat16), preferred_element_type=jnp.float32
    )
    table = jnp.stack(
        [
            jnp.where(chosen, ranking - 1.0, -1.0),
            jnp.sum(jnp.where(named, combine.T[None], 0.0), axis=1),
        ],
        axis=1,
    )
    tables = lax.all_to_all(table, "ctx", split_axis=0, concat_axis=0, tiled=True)

    queries = jnp.transpose(q_latent, (1, 2, 0))
    step = jnp.arange(SQUARE, dtype=jnp.int32)
    others = jnp.concatenate([(plane - by) * SQUARE + (spot ^ step) for by in range(planes)])
    far = jnp.int32(1 << 20)

    def mode_of(block, tokens, low, high):
        limit = jnp.where(others == here, block * tokens, jnp.where(others < here, far, -far))
        seen = jnp.clip(plane + 1 - low, 0, high - low)
        tail = jnp.stack([jnp.int32(block), seen])
        return jnp.concatenate([limit[low * SQUARE : high * SQUARE], tail]).astype(jnp.int32)

    def project(made):
        return lax.dot_general(
            made, w_out, (((0,), (0,)), ((), ())), preferred_element_type=jnp.float32
        )

    if group == 2 and rows % LANES == 0 and planes > 1:
        side = lax.axis_index("head") * sizes["ep"] + lax.axis_index("ep")
        halves = {"other": 1 - side, "own": side}
        near, distant = key_blocks[:SQUARE], key_blocks[SQUARE:]
        cuts = {"other": 2 if heads_here % 4 == 0 else 1, "own": 1}
        states = {
            which: [
                attend(
                    queries,
                    near,
                    mode_of(block, rows, 0, 1),
                    w_value,
                    rows,
                    last=False,
                    part=part,
                    parts=cuts[which],
                )
                for part in range(cuts[which])
            ]
            for which, block in halves.items()
        }

        def finish(which):
            mode = mode_of(halves[which], rows, 1, planes)
            return attend(queries, distant, mode, w_value, rows, states[which])

        partial = project(finish("other")).astype(jnp.bfloat16)
        came = lax.ppermute(partial, ("head", "ep"), [(0, 1), (1, 0)])
        attended = project(finish("own")) + came.astype(jnp.float32)
    else:
        made = [
            attend(queries, key_blocks, mode_of(b, LANES, 0, planes), w_value, LANES)
            for b in range(tokens_here // LANES)
        ]
        attended = lax.psum_scatter(
            project(jnp.concatenate(made, axis=1)),
            ("head", "ep"),
            scatter_dimension=0,
            tiled=True,
        )
    after_attn = lax.optimization_barrier(
        (resid.astype(jnp.float32) + attended).astype(jnp.bfloat16)
    )
    widened = after_attn.astype(jnp.float32)
    mean_square = jnp.mean(widened * widened, axis=1, keepdims=True)
    normed = (widened * lax.rsqrt(mean_square + norm_epsilon) * norm_gain).astype(jnp.bfloat16)

    arrived, first = [], normed
    for n in range(planes):
        if n:
            first = shift(first, 1)
        across = swap(first, 2)
        beside = swap(first, 1)
        corner = swap(across, 1)
        arrived.append([[first], [across], [beside], [corner]])

    capacity = 5 * rows * TOPK // (4 * count)
    slots = -(-capacity // 16) * 16
    rank = tables[:, 0].astype(jnp.int32)
    weight = tables[:, 1]

    carried = summed = None
    for n in list(range(1, planes)) + [0]:
        order = (plane - n) % planes * SQUARE + (spot ^ jnp.array([0, 2, 1, 3], jnp.int32))
        kept, sent = experts(arrived[n], shards, rank[order], weight[order], slots)
        other = swap(sent, 1)
        crossing = (kept[1].astype(jnp.float32) + other[1].astype(jnp.float32)).astype(jnp.bfloat16)
        crossing = swap(crossing, 2)
        summed = kept[0].astype(jnp.float32) + other[0].astype(jnp.float32) + crossing.astype(jnp.float32)
        if carried is not None:
            summed = summed + carried.astype(jnp.float32)
        if n:
            carried = shift(summed.astype(jnp.bfloat16), 1)
    return (widened + routed_factor * summed).astype(jnp.bfloat16)


def solution(mesh):
    placed = (
        P("ctx", ("head", "ep"), None),
        P("ctx", None),
        P(("head", "ep"), None, None),
        P(("head", "ep"), None),
        P(("ctx", "head", "ep"), None),
        P(),
        P("ctx", None, "head"),
        P("ctx", None, "head"),
        P("ctx", None, "head"),
        P(("ctx", "head", "ep"), None),
        P(("ctx", "head", "ep"), None),
    )

    def body(*arguments):
        return per_device(dict(mesh.shape), *arguments)

    return jax.shard_map(
        body,
        mesh=mesh,
        in_specs=placed,
        out_specs=P(("ctx", "head", "ep"), None),
        check_vma=False,
    )
```
